32 devices in a mesh: phase: 2 (over core), dp: 16 (over z, y, x).
Axes of the slice: x: 2, y: 2, z: 4, core: 2. Of those that a mesh axis runs over, the one named last changes fastest.
Arguments:
- tokens: bfloat16 [2, 1536, 1280], P(None, 'dp'), may hold values from -6 to 6
- segment_ids: int32 [2, 1536], replicated, may hold values from 0 to 3, as said below
- loss_mask: int32 [2, 1536], P(None, 'dp'), may hold values 0 or 1
- qkv_weight: bfloat16 [2, 1280, 3840], P('phase', 'dp'), may hold values from -0.15625 to 0.15625
- gains: float32 [2, 1280], P('phase'), may hold values from 0.5 to 1.5
- cotangent: bfloat16 [2, 1536, 1280], P(None, 'dp'), may hold values from -6 to 6
Outputs:
- boundary: bfloat16 [2, 2, 1536, 1280], P('phase', None, 'dp')
- gain_grad: float32 [2, 1280], P('phase', 'dp')
The draws below stay inside these ranges and needn't reach their ends.
Inputs may be any that keep to these rules, and one draw needn't show every extreme that they name: `segment_ids`: in each micro-batch the label is 0 at the first token and moves on by one, modulo 4, at the first token of each MSA sequence; it never changes elsewhere.
All inputs are finite; a program needn't handle non-finite values. No bound on the sum of `loss_mask` on one device may be relied on, other than what follows from the above.
Results may differ from the reference program's by a relative error of at most 0.014.
Values may be sent and summed in bfloat16 or wider, within the bound.
No kernel may reach another device: no remote copies, remote signals or barrier semaphores. Data moves between devices by JAX's collectives and lax.ppermute only.
A program may use at most 128 MiB of HBM per device.

```python
import math
import jax
import jax.numpy as jnp
from jax import lax

WIDTH = 1280
HEADS = 16
HEAD_DIM = 80
MICRO = 2
TOK_DEV = 96
TOKENS = 1536


def draw_segment_ids(key, part):
    starts = jax.random.randint(jax.random.fold_in(key, 17), (MICRO, TOKENS), 0, 64) == 0
    overall = jnp.arange(TOKENS, dtype=jnp.int32)
    micro_rows = jnp.arange(MICRO, dtype=jnp.int32)
    forced = (micro_rows[:, None] == 0) & (overall[None, :] < 2 * TOK_DEV) & (overall[None, :] % (TOK_DEV // 2) == 0)
    starts = starts | (overall[None, :] == 0) | forced
    counted = jnp.cumsum(starts.astype(jnp.int32), axis=-1) - 1
    return (counted % 4).astype(jnp.int32)


def plant(values, rng, smallest, high):
    extent = values.shape
    place = [jax.random.randint(jax.random.fold_in(rng, axis), (), 0, extent[axis]) for axis in range(len(extent))]
    values = values.at[tuple(place)].set(smallest)
    longest = extent.index(max(extent))
    place[longest] = (place[longest] + 1) % extent[longest]
    return values.at[tuple(place)].set(high)


def strengthened(entries, stream_key, source, target, blocks, factor):
    def block_of(axis_at):
        return (jnp.arange(entries.shape[axis_at]) // (entries.shape[axis_at] // blocks)).reshape((-1,) + (1,) * (entries.ndim - 1 - axis_at))

    one_side = jax.random.permutation(stream_key, blocks)[block_of(target)]
    second = (block_of(target) + blocks // 2) % blocks
    return jnp.where((block_of(source) == one_side) | (block_of(source) == second), factor * entries, entries)


def shard_levels(rng, shape, pieces, least, largest):
    loudness = 1.0
    for axis_at, parts in pieces:
        heights = jax.random.uniform(jax.random.fold_in(jax.random.fold_in(rng, 6), axis_at), (parts,), jnp.float32, least / len(pieces), largest / len(pieces))
        loudness = loudness * jnp.repeat(jnp.exp(heights), shape[axis_at] // parts).reshape((-1,) + (1,) * (len(shape) - 1 - axis_at))
    return loudness


def centred(own_key, shape, spread, limit, shards=(), held_as=jnp.bfloat16):
    entries = jax.random.normal(own_key, shape, jnp.float32) * spread
    if len(shards) > 0:
        entries = shard_levels(own_key, shape, shards, -0.22, 0.18) * entries
    return jnp.clip(entries, min=-limit, max=limit).astype(held_as)


def gaussian_with(key, shape, spread, most, split, heavy, kind=jnp.bfloat16):
    values = spread * jax.random.normal(key, shape, jnp.float32)
    if split:
        values = values * shard_levels(key, shape, split, -0.22, 0.18)
    return jnp.clip(strengthened(values, jax.random.fold_in(key, 3), *heavy), -most, most).astype(kind)


def setup_inputs(seed: int = 0) -> dict:
    keys = jax.random.split(jax.random.key(seed), 7)
    return {
        "tokens": centred(keys[0], (MICRO, TOKENS, WIDTH), 1.0, 6.0, ((1, 16),)),
        "segment_ids": draw_segment_ids(jax.random.fold_in(keys[6], 71), 0),
        "loss_mask": plant((jax.random.randint(keys[2], (MICRO, TOKENS), 0, 3) < 1).astype(jnp.int32), jax.random.fold_in(keys[2], 1), 0, 1),
        "qkv_weight": centred(keys[3], (2, WIDTH, 3 * WIDTH), WIDTH ** -0.5, 0.15625, ((0, 2), (1, 16))),
        "gains": jnp.clip(1.0 + 0.1 * jax.random.normal(keys[4], (2, WIDTH), jnp.float32), 0.5, 1.5),
        "cotangent": gaussian_with(keys[5], (MICRO, TOKENS, WIDTH), 1.0, 6.0, ((1, 16),), (1, 2, 16, 2.0)),
    }


def normalize(inputs, scaling):
    widened = inputs.astype(jnp.float32)
    inverse = lax.rsqrt(lax.optimization_barrier(jnp.mean(widened * widened, axis=-1, keepdims=True)) + 1e-05)
    normed = (widened * inverse * scaling).astype(jnp.bfloat16)
    return (widened, inverse, normed)

def windows(project, labels):
    count = TOKENS // TOK_DEV
    shaped = project.reshape(count, TOK_DEV, 3, HEADS, HEAD_DIM)
    pairs = shaped[:, :, 1:]
    remote_pairs = jnp.concatenate([jnp.zeros_like(pairs[:1]), pairs[:-1]], axis=0)
    runs = labels.reshape(count, TOK_DEV)
    remote_runs = jnp.concatenate([runs[:1], runs[:-1]], axis=0)
    order = jnp.arange(count, dtype=jnp.int32)
    return (shaped, remote_pairs, runs, remote_runs, order)

def span_probs(shaped, remote_pairs, run_q, run_r, order):
    local = shaped.astype(jnp.float32)
    remote = remote_pairs.astype(jnp.float32)
    queries = local[:, 0]
    key_rows = jnp.concatenate([remote[:, 0], local[:, 1]], axis=0)
    values = jnp.concatenate([remote[:, 1], local[:, 2]], axis=0)
    position = jnp.arange(TOK_DEV)
    local_ok = (run_q[:, None] == run_q[None, :]) & (position[None, :] <= position[:, None])
    remote_ok = (run_q[:, None] == run_r[None, :]) & (order > 0)
    allowed = jnp.concatenate([remote_ok, local_ok], axis=1)
    scores = jnp.einsum('qhd,khd->hqk', queries, key_rows) / math.sqrt(HEAD_DIM)
    scores = jnp.where(allowed[None], scores, -1e+30)
    highest = lax.optimization_barrier(jnp.max(scores, axis=-1, keepdims=True))
    exponent = jnp.exp(scores - highest)
    softmax = exponent / lax.optimization_barrier(jnp.sum(exponent, axis=-1, keepdims=True))
    return (queries, key_rows, values, softmax)

def section_forward(inputs, labels, scaling, weight):
    widened, inverse, normed = normalize(inputs, scaling)
    project = jnp.dot(normed, weight, preferred_element_type=jnp.float32).astype(jnp.bfloat16)

    def one_run(group):
        queries, key_rows, values, softmax = span_probs(*group)
        rounded = lax.optimization_barrier(softmax.astype(jnp.bfloat16)).astype(jnp.float32)
        return jnp.einsum('hqk,khd->qhd', rounded, values).reshape(TOK_DEV, WIDTH)
    attended = lax.map(one_run, windows(project, labels)).reshape(TOKENS, WIDTH)
    return (widened + attended).astype(jnp.bfloat16)

def section_backward(inputs, labels, scaling, weight, upstream):
    widened, inverse, normed = normalize(inputs, scaling)
    project = jnp.dot(normed, weight, preferred_element_type=jnp.float32).astype(jnp.bfloat16)
    flowing = upstream.astype(jnp.float32)
    count = TOKENS // TOK_DEV
    shaped, remote_pairs, runs, remote_runs, order = windows(project, labels)
    flows = flowing.reshape(count, TOK_DEV, HEADS, HEAD_DIM)

    def one_run(group):
        queries, key_rows, values, softmax = span_probs(*group[:5])
        per_head = group[5]
        rounded = lax.optimization_barrier(softmax.astype(jnp.bfloat16)).astype(jnp.float32)
        grad_soft = jnp.einsum('qhd,khd->hqk', per_head, values)
        grad_values = jnp.einsum('hqk,qhd->khd', rounded, per_head)
        grad_scores = softmax * (grad_soft - lax.optimization_barrier(jnp.sum(softmax * grad_soft, axis=-1, keepdims=True))) / math.sqrt(HEAD_DIM)
        grad_queries = jnp.einsum('hqk,khd->qhd', grad_scores, key_rows)
        grad_keys = jnp.einsum('hqk,qhd->khd', grad_scores, queries)
        return (grad_queries.reshape(TOK_DEV, WIDTH), grad_keys.reshape(2 * TOK_DEV, WIDTH), grad_values.reshape(2 * TOK_DEV, WIDTH))
    grad_q, grad_k, grad_v = lax.map(one_run, (shaped, remote_pairs, runs, remote_runs, order, flows))
    zero_run = jnp.zeros((1, TOK_DEV, WIDTH), jnp.float32)
    own_k = grad_k[:, TOK_DEV:] + jnp.concatenate([grad_k[1:, :TOK_DEV], zero_run], axis=0)
    own_v = grad_v[:, TOK_DEV:] + jnp.concatenate([grad_v[1:, :TOK_DEV], zero_run], axis=0)
    grad_project = jnp.concatenate([grad_q.reshape(TOKENS, WIDTH), own_k.reshape(TOKENS, WIDTH), own_v.reshape(TOKENS, WIDTH)], axis=1).astype(jnp.bfloat16)
    grad_normed = jnp.dot(grad_project, weight.T, preferred_element_type=jnp.float32)
    grad_gain = lax.optimization_barrier(jnp.sum(grad_normed * widened * inverse, axis=0))
    scaled = grad_normed * scaling
    grad_inputs = inverse * (scaled - widened * inverse * inverse * lax.optimization_barrier(jnp.mean(scaled * widened, axis=-1, keepdims=True)))
    return ((flowing + grad_inputs).astype(jnp.bfloat16), grad_gain)

def reference(tokens, segment_ids, loss_mask, qkv_weight, gains, cotangent):
    outputs = []
    gradients = []
    first_total = jnp.zeros((WIDTH,), jnp.float32)
    second_total = jnp.zeros((WIDTH,), jnp.float32)
    for micro_index in range(MICRO):
        entering = tokens[micro_index]
        labels = segment_ids[micro_index]
        middle = section_forward(entering, labels, gains[0], qkv_weight[0])
        final = section_forward(middle, labels, gains[1], qkv_weight[1])
        selected = loss_mask[micro_index][:, None] == 1
        upstream = jnp.where(selected, cotangent[micro_index], jnp.zeros((), jnp.bfloat16))
        back_middle, gain_second = section_backward(middle, labels, gains[1], qkv_weight[1], upstream)
        back_first, gain_first = section_backward(entering, labels, gains[0], qkv_weight[0], back_middle)
        outputs.append(final)
        gradients.append(back_first)
        first_total = first_total + gain_first
        second_total = second_total + gain_second
    boundary = jnp.stack([jnp.stack(gradients), jnp.stack(outputs)])
    return (boundary, jnp.stack([first_total, second_total]))
```

```python
import functools
import math

import jax
import jax.numpy as jnp
from jax import lax
from jax.experimental import pallas as pl
from jax.experimental.pallas import tpu as pltpu
from jax.sharding import PartitionSpec as P

HEADS = 16
HEAD_DIM = 80
LANES = 128
NEGATIVE = -1e30
SCALE = 1.0 / math.sqrt(HEAD_DIM)


def passed_along(x, axis, by):
    size = lax.axis_size(axis)
    pairs = [(i, i + by) for i in range(size) if 0 <= i + by < size]
    return lax.ppermute(x, axis, pairs)


def traded(x, axis, mask):
    return lax.ppermute(x, axis, [(i, i ^ mask) for i in range(lax.axis_size(axis))])


def gathered(shard, axis):
    size = lax.axis_size(axis)
    rows = shard.shape[0]
    if size & (size - 1) or size < 4 or rows % 16:
        return [(lax.all_gather(shard, axis, axis=0, tiled=True), None)]
    bits = [1 << b for b in range(size.bit_length() - 1)]
    first, last = bits[2:][::-1], bits[:2]
    held, masks = shard, [0]
    parts = [(held, masks)]
    for at, bit in enumerate(first):
        other = traded(held, axis, bit)
        if at + 1 < len(first):
            held = jnp.concatenate([held, other], axis=0)
            masks = masks + [m ^ bit for m in masks]
            parts = [(held, masks)]
        else:
            parts = [(held, masks), (other, [m ^ bit for m in masks])]
    near, far = last
    found = list(parts)
    for at, (held, masks) in enumerate(parts):
        a = traded(held, axis, near)
        b = traded(held, axis, far)
        c = traded(a, axis, far) if at % 2 == 0 else traded(b, axis, near)
        found.append((a, [m ^ near for m in masks]))
        found.append((b, [m ^ far for m in masks]))
        found.append((c, [m ^ near ^ far for m in masks]))
    return found


def window(head, width):
    start = min(head * HEAD_DIM // LANES * LANES, width - 2 * LANES)
    lane = lax.broadcasted_iota(jnp.int32, (1, 2 * LANES), 1) + start
    own = (lane >= head * HEAD_DIM) & (lane < (head + 1) * HEAD_DIM)
    return slice(start, start + 2 * LANES), own


def only(own, x):
    return jnp.where(own, x, jnp.zeros((), x.dtype))


def dot(a, b, over):
    return lax.dot_general(a, b, (((over[0],), (over[1],)), ((), ())), preferred_element_type=jnp.float32)


def fetch(plan, refs, weight, sem, place, phase, rows):
    copies = []
    for at, (ref, (masks, mine)) in enumerate(zip(refs, plan)):
        half = phase if mine else 1 - phase
        if masks is None:
            copies.append(pltpu.make_async_copy(ref, weight.at[half], sem.at[len(copies)]))
            continue
        for block, mask in enumerate(masks):
            start = pl.multiple_of((place ^ mask) * rows, 16)
            copies.append(
                pltpu.make_async_copy(
                    ref.at[pl.ds(block * rows, rows)], weight.at[half, pl.ds(start, rows)], sem.at[len(copies)]
                )
            )
    return copies


def copy_count(plan):
    return sum(1 if masks is None else len(masks) for masks, _ in plan)


def bias_of(column, row, has_left, length):
    key = lax.broadcasted_iota(jnp.int32, (2 * length, length), 0) - length
    query = lax.broadcasted_iota(jnp.int32, (2 * length, length), 1)
    ok = (column == row) & (key <= query) & ((key >= 0) | has_left)
    return jnp.where(ok, 0.0, NEGATIVE)


def softmax_of(q, k, bias):
    scores = dot(k, q, (1, 1)) * SCALE + bias
    exponent = jnp.exp(scores - jnp.max(scores, axis=0, keepdims=True))
    return exponent * (1.0 / jnp.sum(exponent, axis=0, keepdims=True))


def normalized(x, gain):
    wide = x.astype(jnp.float32)
    inverse = lax.rsqrt(jnp.mean(wide * wide, axis=-1, keepdims=True) + 1e-05)
    return wide, inverse, (wide * inverse * gain).astype(jnp.bfloat16)


def projected(normed, weight, proj, step):
    half = weight.shape[2]
    for h in range(2):

        def tile(n, _, h=h):
            at = pl.multiple_of(n * step, LANES)
            product = jnp.dot(normed[...], weight[h, :, pl.ds(at, step)], preferred_element_type=jnp.float32)
            proj[:, pl.ds(pl.multiple_of(h * half + at, LANES), step)] = product.astype(jnp.bfloat16)
            return 0

        lax.fori_loop(0, half // step, tile, 0)


def forward_kernel(plan, shard_rows, runs, *refs):
    count = len(plan)
    at_ref, x_ref, column_ref, row_ref, gain_ref = refs[:5]
    pieces = refs[5 : 5 + count]
    out_ref, proj_ref = refs[5 + count : 7 + count]
    weight, normed_ref, sem = refs[7 + count :]
    phase, place = at_ref[0], at_ref[1]
    copies = fetch(plan, pieces, weight, sem, place, phase, shard_rows)
    for c in copies:
        c.start()
    length = x_ref.shape[0] // runs
    width = x_ref.shape[1]
    _, _, normed = normalized(x_ref[...], gain_ref[...])
    normed_ref[...] = normed
    for c in copies:
        c.wait()
    projected(normed_ref, weight, proj_ref, width // 2)

    def one_run(i, _):
        base = pl.multiple_of(i * length, 16)
        before = pl.multiple_of((i - 1) * length, 16)
        bias = bias_of(
            column_ref[pl.ds(before, 2 * length)], row_ref[i], place + i - runs // 2 > 0, length
        )
        total = [jnp.zeros((length, LANES), jnp.float32) for _ in range(width // LANES)]
        for head in range(HEADS):
            cols, own = window(head, width)
            q = only(own, proj_ref[pl.ds(base, length), cols])
            k = proj_ref[pl.ds(before, 2 * length), width + cols.start : width + cols.stop]
            v = proj_ref[pl.ds(before, 2 * length), 2 * width + cols.start : 2 * width + cols.stop]
            soft = softmax_of(q, k, bias)
            part = dot(soft.astype(jnp.bfloat16), only(own, v), (0, 0))
            t = cols.start // LANES
            total[t] = total[t] + part[:, :LANES]
            total[t + 1] = total[t + 1] + part[:, LANES:]
        for t in range(width // LANES):
            lanes = slice(t * LANES, (t + 1) * LANES)
            x = x_ref[pl.ds(base, length), lanes].astype(jnp.float32)
            out_ref[pl.ds(before, length), lanes] = (x + total[t]).astype(jnp.bfloat16)
        return 0

    lax.fori_loop(1, runs, one_run, 0)


def backward_kernel(plan, shard_rows, runs, first_run, fresh, *refs):
    count = len(plan)
    at_ref, x_ref, g_ref, column_ref, row_ref, gain_ref = refs[:6]
    pieces = refs[6 : 6 + count]
    refs = refs[6 + count :]
    if fresh:
        grad_ref, term_ref, out_ref, weight, proj_ref, normed_ref, dq, dk, dv, total, sem = refs
    else:
        proj_ref, grad_ref, term_ref, weight, dq, dk, dv, total, sem = refs
    phase, place = at_ref[0], at_ref[1]
    copies = fetch(plan, pieces, weight, sem, place, phase, shard_rows)
    for c in copies:
        c.start()
    length = x_ref.shape[0] // runs
    width = x_ref.shape[1]
    outs = (runs - 2) * length
    if fresh:
        normed_ref[...] = normalized(x_ref[...], gain_ref[...])[2]
        for c in copies:
            c.wait()
        projected(normed_ref, weight, proj_ref, width // 2)
    dq[...] = jnp.zeros_like(dq)
    dk[...] = jnp.zeros_like(dk)
    dv[...] = jnp.zeros_like(dv)

    def one_run(i, attend):
        base = pl.multiple_of(i * length, 16)
        before = pl.multiple_of((i - 1) * length, 16)
        queries, keys = pl.ds(base, length), pl.ds(before, 2 * length)
        bias = bias_of(column_ref[keys], row_ref[i], place + i + first_run > 0, length)
        attended = [jnp.zeros((length, LANES), jnp.float32) for _ in range(width // LANES)] if attend else None
        for head in range(HEADS):
            cols, own = window(head, width)
            q = only(own, proj_ref[queries, cols])
            k = proj_ref[keys, width + cols.start : width + cols.stop]
            v = proj_ref[keys, 2 * width + cols.start : 2 * width + cols.stop]
            g = only(own, g_ref[pl.ds(before, length), cols])
            soft = softmax_of(q, k, bias)
            rounded = soft.astype(jnp.bfloat16)
            if attend:
                part = dot(rounded, only(own, v), (0, 0))
                t = cols.start // LANES
                attended[t] = attended[t] + part[:, :LANES]
                attended[t + 1] = attended[t + 1] + part[:, LANES:]
            grad_soft = dot(v, g, (1, 1))
            weighed = soft * grad_soft
            grad_scores = (weighed - soft * jnp.sum(weighed, axis=0, keepdims=True)) * SCALE
            grad_scores = grad_scores.astype(jnp.bfloat16)
            dv[keys, cols] += dot(rounded, g, (1, 0))
            dk[keys, cols] += dot(grad_scores, q, (1, 0))
            dq[pl.ds(before, length), cols] += dot(grad_scores, only(own, k), (0, 0))
        if attend:
            for t in range(width // LANES):
                lanes = slice(t * LANES, (t + 1) * LANES)
                x = x_ref[queries, lanes].astype(jnp.float32)
                out_ref[:, lanes] = (x + attended[t]).astype(jnp.bfloat16)

    def looped(i, _):
        one_run(i, False)
        return 0

    if fresh:
        one_run(1, True)
        lax.fori_loop(2, runs, looped, 0)
    else:
        lax.fori_loop(1, runs, looped, 0)
        for c in copies:
            c.wait()

    half = weight.shape[2]
    step = width // 2
    for tile in range(3 * width // step):
        source, column = divmod(tile * step, width)
        grads = (dq[0:outs], dk[length : length + outs], dv[length : length + outs])[source]
        product = dot(
            grads[:, column : column + step].astype(jnp.bfloat16),
            weight[tile * step // half, :, tile * step % half : tile * step % half + step],
            (1, 1),
        )
        if tile == 0:
            total[...] = product
        else:
            total[...] += product
    wide, inverse, _ = normalized(x_ref[length : length + outs], gain_ref[...])
    grad_normed = total[...]
    term_ref[...] = jnp.sum(
        grad_normed[:length] * wide[:length] * inverse[:length], axis=0, keepdims=True
    )
    scaled = grad_normed * gain_ref[...]
    inner = jnp.mean(scaled * wide, axis=-1, keepdims=True)
    grads = inverse * (scaled - wide * inverse * inverse * inner)
    grad_ref[...] = (g_ref[0:outs].astype(jnp.float32) + grads).astype(jnp.bfloat16)


def specs(*kinds):
    spaces = {"s": pltpu.SMEM, "v": pltpu.VMEM, "a": pl.ANY}
    return [pl.BlockSpec(memory_space=spaces[k]) for k in kinds]


def flattened(found):
    arrays, plan = [], []
    for array, masks in found:
        arrays.append(array)
        plan.append((masks, True))
    for array, masks in found:
        arrays.append(traded(array, "phase", 1))
        plan.append((masks, False))
    return arrays, plan


def shards(tokens, segment_ids, loss_mask, qkv_weight, gains, cotangent):
    length, width = tokens.shape[1:]
    phase = lax.axis_index("phase")
    place = lax.axis_index("dp")
    shard_rows, columns = qkv_weight.shape[1:]
    half = columns // 2
    first = phase == 0
    lo, hi = qkv_weight[0, :, :half], qkv_weight[0, :, half:]
    swapped = traded(jnp.where(first, hi, lo), "phase", 1)
    w0, plan0 = flattened(gathered(jnp.where(first, lo, swapped), "dp"))
    w1, plan1 = flattened(gathered(jnp.where(first, swapped, hi), "dp"))

    mine = lambda a: jnp.where(first, a[0], a[1])
    x = mine(tokens)
    g2 = jnp.where(mine(loss_mask)[:, None] == 1, mine(cotangent), jnp.zeros((), jnp.bfloat16))
    both = jnp.concatenate([x, g2], axis=0)
    right1 = passed_along(both, "dp", -1)
    right2 = passed_along(both, "dp", -2)
    runs = 5
    wide = jnp.concatenate(
        [passed_along(x, "dp", 2), passed_along(x, "dp", 1), x, right1[:length], right2[:length]], axis=0
    )
    upstream = jnp.concatenate([g2, right1[length:], right2[length:]], axis=0)
    labels = lax.dynamic_slice_in_dim(jnp.pad(mine(segment_ids), 2 * length), place * length, runs * length)
    column = labels[:, None]
    row = labels.reshape(runs, 1, length)
    other = traded(gains, "phase", 1)
    gain0, gain1 = jnp.where(first, gains, other), jnp.where(first, other, gains)
    at = jnp.stack([phase, place]).astype(jnp.int32)
    limit = pltpu.CompilerParams(vmem_limit_bytes=60 * 1024 * 1024)
    bf16, f32 = jnp.bfloat16, jnp.float32
    weight_scratch = pltpu.VMEM((2, width, half), bf16)
    matmul = 2 * width * columns

    h1, proj0 = pl.pallas_call(
        functools.partial(forward_kernel, plan0, shard_rows, runs),
        out_shape=(
            jax.ShapeDtypeStruct(((runs - 1) * length, width), bf16),
            jax.ShapeDtypeStruct((runs * length, columns), bf16),
        ),
        in_specs=specs(*"svvvv", *("a" * len(w0))),
        out_specs=tuple(specs(*"vv")),
        scratch_shapes=[
            weight_scratch,
            pltpu.VMEM((runs * length, width), bf16),
            pltpu.SemaphoreType.DMA((copy_count(plan0),)),
        ],
        compiler_params=limit,
        cost_estimate=pl.CostEstimate(
            flops=2 * matmul * runs * length, bytes_accessed=2 * width * columns, transcendentals=0
        ),
        name="forward0",
    )(at, wide, column, row, gain0, *w0)

    def backward(runs, skip, x, g, gain, weights, plan, proj):
        rows = slice(skip * length, (skip + runs) * length)
        fresh = proj is None
        outs = (runs - 2) * length
        shapes = [jax.ShapeDtypeStruct((outs, width), bf16), jax.ShapeDtypeStruct((1, width), f32)]
        scratch = [weight_scratch]
        if fresh:
            shapes.append(jax.ShapeDtypeStruct((length, width), bf16))
            scratch += [pltpu.VMEM((runs * length, columns), bf16), pltpu.VMEM((runs * length, width), bf16)]
        scratch += [
            pltpu.VMEM(((runs - 1) * length, width), f32),
            pltpu.VMEM((runs * length, width), f32),
            pltpu.VMEM((runs * length, width), f32),
            pltpu.VMEM((outs, width), f32),
            pltpu.SemaphoreType.DMA((copy_count(plan),)),
        ]
        return pl.pallas_call(
            functools.partial(backward_kernel, plan, shard_rows, runs, skip - 2, fresh),
            out_shape=tuple(shapes),
            in_specs=specs(*"svvvvv", *("a" * len(weights)), *("" if fresh else "v")),
            out_specs=tuple(specs(*("v" * len(shapes)))),
            scratch_shapes=scratch,
            compiler_params=limit,
            cost_estimate=pl.CostEstimate(
                flops=2 * matmul * runs * length, bytes_accessed=2 * width * columns, transcendentals=0
            ),
            name="backward1" if fresh else "backward0",
        )(at, x, g, column[rows], row[skip : skip + runs], gain, *weights, *(() if fresh else (proj,)))

    g1, term1, out = backward(4, 1, h1, upstream, gain1, w1, plan1, None)
    g0, term0 = backward(
        3, 1, wide[length : 4 * length], g1, gain0, w0, plan0, proj0[length : 4 * length]
    )
    received = traded(jnp.where(first, out, g0), "phase", 1)
    boundary = jnp.where(first, jnp.stack([g0, received]), jnp.stack([received, out]))[None]
    terms = jnp.where(first, term0, term1) + traded(jnp.where(first, term1, term0), "phase", 1)
    size = lax.axis_size("dp")
    if size & (size - 1):
        return boundary, lax.psum_scatter(terms, "dp", scatter_dimension=1, tiled=True)
    terms = terms.reshape(size, width // size)
    bit = size // 2
    while bit:
        upper = (place & bit) != 0
        low, high = terms[:bit], terms[bit:]
        terms = jnp.where(upper, high, low) + traded(jnp.where(upper, low, high), "dp", bit)
        bit //= 2
    return boundary, terms


def solution(mesh):
    in_specs = (
        P(None, "dp", None),
        P(),
        P(None, "dp"),
        P("phase", "dp", None),
        P("phase", None),
        P(None, "dp", None),
    )
    out_specs = (P("phase", None, "dp", None), P("phase", "dp"))
    return jax.shard_map(shards, mesh=mesh, in_specs=in_specs, out_specs=out_specs, check_vma=False)
```

```python
import functools
import math

import jax
import jax.numpy as jnp
from jax import lax
from jax.experimental import pallas as pl
from jax.experimental.pallas import tpu as pltpu
from jax.sharding import PartitionSpec as P


HEADS = 16
HEAD_DIM = 80
LANES = 128
NEGATIVE = -1e30
SCALE = 1.0 / math.sqrt(HEAD_DIM)


def passed_along(x, axis, by):
    size = lax.axis_size(axis)
    return lax.ppermute(x, axis, [(i, (i + by) % size) for i in range(size)])


def traded(x, axis, mask):
    return lax.ppermute(x, axis, [(i, i ^ mask) for i in range(lax.axis_size(axis))])


def gathered(shard, axis, cut, swap):
    size = lax.axis_size(axis)
    rows = shard.shape[0]
    if size & (size - 1) or size < 8 or rows % 16:
        return [(lax.all_gather(shard, axis, axis=0, tiled=True), None, 0)]
    bits = [1 << b for b in range(size.bit_length() - 1)]
    line, (near, far) = bits[2:][::-1], bits[:2][::-1] if swap else bits[:2]

    def along(blocks):
        found = [(blocks, 0)]
        for bit in line:
            found += [(traded(b, axis, bit), m ^ bit) for b, m in found]
        return found[1:]

    def across(blocks):
        a = traded(blocks, axis, near)
        b = traded(blocks, axis, far)
        return [(a, near), (b, far), (traded(b, axis, near), near ^ far)]

    lines = along(shard)
    plane = across(shard)
    stacked = jnp.concatenate([b for b, _ in lines], axis=0)
    masks = [m for _, m in lines]
    around = jnp.concatenate([shard] + [b for b, _ in plane], axis=0)
    plane_masks = [m for _, m in plane]
    found = [(around, [0] + plane_masks, 0), (stacked, masks, 0)]
    if cut < shard.shape[1]:
        found += [(b, [m ^ p for p in plane_masks], cut) for b, m in along(around[rows:, cut:])]
        stacked = stacked[:, :cut]
    a, b = traded(stacked, axis, near), traded(stacked, axis, far)
    middle = cut // 2 // LANES * LANES
    both = [m ^ near ^ far for m in masks]
    found += [(a, [m ^ near for m in masks], 0), (b, [m ^ far for m in masks], 0)]
    if cut < shard.shape[1]:
        return found + [(traded(stacked, axis, near ^ far), both, 0)]
    found.append((traded(b[:, :middle], axis, near), both, 0))
    found.append((traded(a[:, middle:], axis, far), both, middle))
    return found


def window(head, width):
    start = min(head * HEAD_DIM // LANES * LANES, width - 2 * LANES)
    lane = lax.broadcasted_iota(jnp.int32, (1, 2 * LANES), 1) + start
    own = (lane >= head * HEAD_DIM) & (lane < (head + 1) * HEAD_DIM)
    return slice(start, start + 2 * LANES), own


def only(own, x):
    return jnp.where(own, x, jnp.zeros((), x.dtype))


def dot(a, b, over):
    return lax.dot_general(a, b, (((over[0],), (over[1],)), ((), ())), preferred_element_type=jnp.float32)


def fetch(plan, refs, weight, sem, place, phase, rows):
    copies = []
    for ref, (masks, column, mine) in zip(refs, plan):
        half = phase if mine else 1 - phase
        cols = pl.ds(column, ref.shape[1])
        if masks is None:
            copies.append(pltpu.make_async_copy(ref, weight.at[half, :, cols], sem.at[len(copies)]))
            continue
        for block, mask in enumerate(masks):
            start = pl.multiple_of((place ^ mask) * rows, 16)
            copies.append(
                pltpu.make_async_copy(
                    ref.at[pl.ds(block * rows, rows)],
                    weight.at[half, pl.ds(start, rows), cols],
                    sem.at[len(copies)],
                )
            )
    return copies


def copy_count(plan):
    return sum(1 if masks is None else len(masks) for masks, _, _ in plan)


def bias_of(column, row, run, last, length):
    key = lax.broadcasted_iota(jnp.int32, (2 * length, length), 0) - length
    query = lax.broadcasted_iota(jnp.int32, (2 * length, length), 1)
    ok = (column == row) & (key <= query) & ((key >= 0) | ((run > 0) & (run <= last)))
    return jnp.where(ok, 0.0, NEGATIVE)


def softmax_of(scores, bias):
    scores = scores * SCALE + bias
    exponent = jnp.exp(scores - jnp.max(scores, axis=0, keepdims=True))
    return exponent * (1.0 / jnp.sum(exponent, axis=0, keepdims=True))


def normalized(x, gain):
    wide = x.astype(jnp.float32)
    inverse = lax.rsqrt(jnp.mean(wide * wide, axis=-1, keepdims=True) + 1e-05)
    return wide, inverse, (wide * inverse * gain).astype(jnp.bfloat16)


def projected(normed, weight, proj, step, copies, plan, phase):
    half = weight.shape[2]
    at = 0
    for mine in (True, False):
        h = phase if mine else 1 - phase
        for masks, _, own in plan:
            if own == mine:
                for _ in range(1 if masks is None else len(masks)):
                    copies[at].wait()
                    at += 1

        def tile(n, _, h=h):
            column = pl.multiple_of(n * step, LANES)
            product = jnp.dot(normed[...], weight[h, :, pl.ds(column, step)], preferred_element_type=jnp.float32)
            proj[:, pl.ds(pl.multiple_of(h * half + column, LANES), step)] = product.astype(jnp.bfloat16)
            return 0

        lax.fori_loop(0, half // step, tile, 0)


def grouped(count=8):
    return [range(h, min(h + count, HEADS)) for h in range(0, HEADS, count)]


def forward_kernel(plan, shard_rows, runs, first_run, *refs):
    count = len(plan)
    at_ref, column_ref, row_ref, gain_ref = refs[:4]
    tokens, pieces = refs[4 : 4 + runs], refs[4 + runs : 4 + runs + count]
    refs = refs[4 + runs + count :]
    outs, kept_ref = refs[: runs - 1], refs[runs - 1]
    weight, proj_ref, normed_ref, total, sem, kept_sem = refs[runs:]
    phase, place = at_ref[0], at_ref[1]
    copies = fetch(plan, pieces, weight, sem, place, phase, shard_rows)
    for c in copies:
        c.start()
    length, width = row_ref.shape[2], weight.shape[1]
    for i in range(runs):
        normed_ref[i * length : (i + 1) * length] = normalized(tokens[i][...], gain_ref[...])[2]
    projected(normed_ref, weight, proj_ref, width // 2, copies, plan, phase)
    keep = pltpu.make_async_copy(proj_ref, kept_ref, kept_sem)
    keep.start()

    for i in range(1, runs):
        queries, keys = slice(i * length, (i + 1) * length), slice((i - 1) * length, (i + 1) * length)
        here = first_run + 2 + i
        label = slice((here - 1) * length, (here + 1) * length)
        bias = bias_of(column_ref[label], row_ref[here], place + i + first_run, at_ref[2], length)
        total[...] = tokens[i][...].astype(jnp.float32)
        for heads in grouped():
            wins = [window(head, width) for head in heads]
            scores = []
            for cols, own in wins:
                q = only(own, proj_ref[queries, cols])
                scores.append(dot(proj_ref[keys, width + cols.start : width + cols.stop], q, (1, 1)))
            soft = [softmax_of(x, bias).astype(jnp.bfloat16) for x in scores]
            for (cols, own), p in zip(wins, soft):
                v = proj_ref[keys, 2 * width + cols.start : 2 * width + cols.stop]
                total[:, cols] += dot(p, only(own, v), (0, 0))
        outs[i - 1][...] = total[...].astype(jnp.bfloat16)
    keep.wait()


def backward_kernel(plan, shard_rows, runs, first_run, places, fresh, *refs):
    count, given = len(plan), 1 + max(which for which, _ in places)
    at_ref, column_ref, row_ref, gain_ref = refs[:4]
    arrays, pieces = refs[4 : 4 + given], refs[4 + given : 4 + given + count]
    refs = refs[4 + given + count :]
    length = row_ref.shape[2]

    def part(at, cols=slice(None)):
        which, row = places[at]
        return arrays[which][row : row + length, cols]

    if fresh:
        grad_ref, term_ref, out_ref, weight, proj_ref, normed_ref, dq, dk, dv, total, sem = refs
    else:
        proj_ref, grad_ref, term_ref, weight, dq, dk, dv, total, sem = refs
    phase, place = at_ref[0], at_ref[1]
    copies = fetch(plan, pieces, weight, sem, place, phase, shard_rows)
    for c in copies:
        c.start()
    width = weight.shape[1]
    dq[...] = jnp.zeros_like(dq)
    dk[...] = jnp.zeros_like(dk)
    dv[...] = jnp.zeros_like(dv)
    if fresh:
        for i in range(runs):
            normed_ref[i * length : (i + 1) * length] = normalized(part(i), gain_ref[...])[2]
        projected(normed_ref, weight, proj_ref, width // 2, copies, plan, phase)

    for i in range(1, runs):
        inner, last, attend = i > 1, i == runs - 1, fresh and i == 1
        queries, keys = slice(i * length, (i + 1) * length), slice((i - 1) * length, (i + 1) * length)
        upstream = slice((i - 1) * length, i * length)
        lo, hi = (0 if inner else length), (length if last else 2 * length)
        into = slice((i - 2) * length + lo, (i - 2) * length + hi)
        label = slice((first_run + 2 + i - 1) * length, (first_run + 2 + i + 1) * length)
        bias = bias_of(column_ref[label], row_ref[first_run + 2 + i], place + i + first_run, at_ref[2], length)
        if attend:
            total[0:length] = part(i).astype(jnp.float32)
        for heads in grouped():
            wins = [window(head, width) for head in heads]
            staged = []
            for cols, own in wins:
                q = only(own, proj_ref[queries, cols])
                g = only(own, part(runs + i - 1, cols))
                k = proj_ref[keys, width + cols.start : width + cols.stop]
                v = proj_ref[keys, 2 * width + cols.start : 2 * width + cols.stop]
                staged.append((q, g, dot(k, q, (1, 1)), dot(v, g, (1, 1))))
            graded = []
            for q, g, scores, grad_soft in staged:
                soft = softmax_of(scores, bias)
                weighed = soft * grad_soft
                grads = (weighed - soft * jnp.sum(weighed, axis=0, keepdims=True)) * SCALE
                graded.append((q, g, soft.astype(jnp.bfloat16), grads.astype(jnp.bfloat16)))
            for (cols, own), (q, g, soft, grads) in zip(wins, graded):
                dv[into, cols] += dot(soft[lo:hi], g, (1, 0))
                dk[into, cols] += dot(grads[lo:hi], q, (1, 0))
                if not last:
                    k = proj_ref[keys, width + cols.start : width + cols.stop]
                    dq[upstream, cols] += dot(grads, only(own, k), (0, 0))
                if attend:
                    v = proj_ref[keys, 2 * width + cols.start : 2 * width + cols.stop]
                    total[0:length, cols] += dot(soft, only(own, v), (0, 0))
        if attend:
            out_ref[...] = total[0:length].astype(jnp.bfloat16)

    if not fresh:
        for c in copies:
            c.wait()
    half = weight.shape[2]
    step = width // 2
    for tile in range(3 * width // step):
        source, column = divmod(tile * step, width)
        grads = (dq, dk, dv)[source][:, column : column + step].astype(jnp.bfloat16)
        start = tile * step % half
        product = dot(grads, weight[tile * step // half, :, start : start + step], (1, 1))
        if tile == 0:
            total[...] = product
        else:
            total[...] += product
    for i in range(1, runs - 1):
        rows = slice((i - 1) * length, i * length)
        wide, inverse, _ = normalized(part(i), gain_ref[...])
        grad_normed = total[rows]
        if i == 1:
            term_ref[...] = jnp.sum(grad_normed * wide * inverse, axis=0, keepdims=True)
        scaled = grad_normed * gain_ref[...]
        inner = jnp.mean(scaled * wide, axis=-1, keepdims=True)
        grads = inverse * (scaled - wide * inverse * inverse * inner)
        grad_ref[rows] = (part(runs + i - 1).astype(jnp.float32) + grads).astype(jnp.bfloat16)


def specs(*kinds):
    spaces = {"s": pltpu.SMEM, "v": pltpu.VMEM, "a": pl.ANY}
    return [pl.BlockSpec(memory_space=spaces[k]) for k in kinds]


def flattened(found):
    arrays, plan = [], []
    for array, masks, column in found:
        arrays.append(array)
        plan.append((masks, column, True))
    for array, masks, column in found:
        arrays.append(traded(array, "phase", 1))
        plan.append((masks, column, False))
    return arrays, plan


def shards(tokens, segment_ids, loss_mask, qkv_weight, gains, cotangent):
    length, width = tokens.shape[1:]
    phase = lax.axis_index("phase")
    place = lax.axis_index("dp")
    shard_rows, columns = qkv_weight.shape[1:]
    half = columns // 2
    first = phase == 0
    lo, hi = qkv_weight[0, :, :half], qkv_weight[0, :, half:]
    swapped = traded(jnp.where(first, hi, lo), "phase", 1)
    cut = half * 2 // 5 // LANES * LANES
    w0, plan0 = flattened(gathered(jnp.where(first, lo, swapped), "dp", half, False))
    w1, plan1 = flattened(gathered(jnp.where(first, swapped, hi), "dp", cut, True))

    mine = lambda a: jnp.where(first, a[0], a[1])
    x = mine(tokens)
    g2 = jnp.where(mine(loss_mask)[:, None] == 1, mine(cotangent), jnp.zeros((), jnp.bfloat16))
    right, left = passed_along(x, "dp", -1), passed_along(x, "dp", 1)
    upstream = [g2, passed_along(g2, "dp", -1), passed_along(g2, "dp", -2)]
    runs = 5
    labels = lax.dynamic_slice_in_dim(jnp.pad(mine(segment_ids), 2 * length), place * length, runs * length)
    column = labels[:, None]
    row = labels.reshape(runs, 1, length)
    other = traded(gains, "phase", 1)
    gain0, gain1 = jnp.where(first, gains, other), jnp.where(first, other, gains)
    at = jnp.stack([phase, place, jnp.int32(lax.axis_size("dp") - 1)]).astype(jnp.int32)
    limit = pltpu.CompilerParams(vmem_limit_bytes=32 * 1024 * 1024)
    bf16, f32 = jnp.bfloat16, jnp.float32
    weight_scratch = pltpu.VMEM((2, width, half), bf16)
    matmul = 2 * width * columns

    labelled = (column, row)
    estimate = pl.CostEstimate(
        flops=2 * matmul * runs * length, bytes_accessed=2 * width * columns, transcendentals=0
    )
    near = (left, x, right)
    rows = len(near) * length
    h1, h1_next, proj0 = pl.pallas_call(
        functools.partial(forward_kernel, plan0, shard_rows, len(near), -1),
        out_shape=(
            jax.ShapeDtypeStruct((length, width), bf16),
            jax.ShapeDtypeStruct((length, width), bf16),
            jax.ShapeDtypeStruct((rows, columns), bf16),
        ),
        in_specs=specs(*"svvv", *("v" * len(near)), *("a" * len(w0))),
        out_specs=tuple(specs(*"vva")),
        scratch_shapes=[
            weight_scratch,
            pltpu.VMEM((rows, columns), bf16),
            pltpu.VMEM((rows, width), bf16),
            pltpu.VMEM((length, width), f32),
            pltpu.SemaphoreType.DMA((copy_count(plan0),)),
            pltpu.SemaphoreType.DMA,
        ],
        compiler_params=limit,
        cost_estimate=estimate,
        name="forward0",
    )(at, *labelled, gain0, *near, *w0)
    around = [passed_along(h1, "dp", 1), h1, h1_next, passed_along(h1_next, "dp", -1)]

    def backward(runs, arrays, places, gain, weights, plan, proj):
        fresh = proj is None
        outs = (runs - 2) * length
        shapes = [jax.ShapeDtypeStruct((outs, width), bf16), jax.ShapeDtypeStruct((1, width), f32)]
        scratch = [weight_scratch]
        if fresh:
            shapes.append(jax.ShapeDtypeStruct((length, width), bf16))
            scratch += [pltpu.VMEM((runs * length, columns), bf16), pltpu.VMEM((runs * length, width), bf16)]
        scratch += [pltpu.VMEM((outs, width), f32)] * 4
        scratch.append(pltpu.SemaphoreType.DMA((copy_count(plan),)))
        kinds = "svvv" + "v" * len(arrays) + "a" * len(weights) + ("" if fresh else "v")
        return pl.pallas_call(
            functools.partial(backward_kernel, plan, shard_rows, runs, -1, places, fresh),
            out_shape=tuple(shapes),
            in_specs=specs(*kinds),
            out_specs=tuple(specs(*("v" * len(shapes)))),
            scratch_shapes=scratch,
            compiler_params=limit,
            cost_estimate=estimate,
            name="backward1" if fresh else "backward0",
        )(at, *labelled, gain, *arrays, *weights, *(() if fresh else (proj,)))

    places1 = [(which, 0) for which in range(7)]
    g1, term1, out = backward(4, (*around, *upstream), places1, gain1, w1, plan1, None)
    places0 = [(0, 0), (1, 0), (2, 0), (3, 0), (3, length)]
    g0, term0 = backward(3, (*near, g1), places0, gain0, w0, plan0, proj0)
    received = traded(jnp.where(first, out, g0), "phase", 1)
    boundary = jnp.where(first, jnp.stack([g0, received]), jnp.stack([received, out]))[None]
    terms = jnp.where(first, term0, term1) + traded(jnp.where(first, term1, term0), "phase", 1)
    size = lax.axis_size("dp")
    if size & (size - 1):
        return boundary, lax.psum_scatter(terms, "dp", scatter_dimension=1, tiled=True)
    terms = terms.reshape(size, width // size)
    bit = size // 2
    while bit:
        if bit == 1:
            terms, boundary = lax.optimization_barrier((terms, boundary))
        upper = (place & bit) != 0
        low, high = terms[:bit], terms[bit:]
        terms = jnp.where(upper, high, low) + traded(jnp.where(upper, low, high), "dp", bit)
        bit //= 2
    return boundary, terms


def solution(mesh):
    in_specs = (
        P(None, "dp", None),
        P(),
        P(None, "dp"),
        P("phase", "dp", None),
        P("phase", None),
        P(None, "dp", None),
    )
    out_specs = (P("phase", None, "dp", None), P("phase", "dp"))
    return jax.shard_map(shards, mesh=mesh, in_specs=in_specs, out_specs=out_specs, check_vma=False)
```

```python
import functools
import math

import jax
import jax.numpy as jnp
from jax import lax
from jax.experimental import pallas as pl
from jax.experimental.pallas import tpu as pltpu
from jax.sharding import PartitionSpec as P


HEADS = 16
HEAD_DIM = 80
LANES = 128
NEGATIVE = -1e30
SCALE = 1.0 / math.sqrt(HEAD_DIM)


def passed_along(x, axis, by):
    size = lax.axis_size(axis)
    return lax.ppermute(x, axis, [(i, (i + by) % size) for i in range(size)])


def traded(x, axis, mask):
    return lax.ppermute(x, axis, [(i, i ^ mask) for i in range(lax.axis_size(axis))])


def gathered(shard, axis, cut, swap):
    size = lax.axis_size(axis)
    rows = shard.shape[0]
    if size & (size - 1) or size < 8 or rows % 16:
        return [(lax.all_gather(shard, axis, axis=0, tiled=True), None, 0)]
    bits = [1 << b for b in range(size.bit_length() - 1)]
    line, (near, far) = bits[2:][::-1], bits[:2][::-1] if swap else bits[:2]

    def along(blocks):
        found = [(blocks, 0)]
        for bit in line:
            found += [(traded(b, axis, bit), m ^ bit) for b, m in found]
        return found[1:]

    def across(blocks):
        a = traded(blocks, axis, near)
        b = traded(blocks, axis, far)
        return [(a, near), (b, far), (traded(b, axis, near), near ^ far)]

    lines = along(shard)
    plane = across(shard)
    stacked = jnp.concatenate([b for b, _ in lines], axis=0)
    masks = [m for _, m in lines]
    around = jnp.concatenate([shard] + [b for b, _ in plane], axis=0)
    plane_masks = [m for _, m in plane]
    found = [(around, [0] + plane_masks, 0), (stacked, masks, 0)]
    if cut < shard.shape[1]:
        found += [(b, [m ^ p for p in plane_masks], cut) for b, m in along(around[rows:, cut:])]
        stacked = stacked[:, :cut]
    a, b = traded(stacked, axis, near), traded(stacked, axis, far)
    middle = cut // 2 // LANES * LANES
    both = [m ^ near ^ far for m in masks]
    found += [(a, [m ^ near for m in masks], 0), (b, [m ^ far for m in masks], 0)]
    if cut < shard.shape[1]:
        return found + [(traded(stacked, axis, near ^ far), both, 0)]
    found.append((traded(b[:, :middle], axis, near), both, 0))
    found.append((traded(a[:, middle:], axis, far), both, middle))
    return found


def window(head, width):
    start = min(head * HEAD_DIM // LANES * LANES, width - 2 * LANES)
    lane = lax.broadcasted_iota(jnp.int32, (1, 2 * LANES), 1) + start
    own = (lane >= head * HEAD_DIM) & (lane < (head + 1) * HEAD_DIM)
    return slice(start, start + 2 * LANES), own


def only(own, x):
    return jnp.where(own, x, jnp.zeros((), x.dtype))


def dot(a, b, over):
    return lax.dot_general(a, b, (((over[0],), (over[1],)), ((), ())), preferred_element_type=jnp.float32)


def fetch(plan, refs, weight, sem, place, phase, rows):
    copies = []
    for ref, (masks, column, mine) in zip(refs, plan):
        half = phase if mine else 1 - phase
        cols = pl.ds(column, ref.shape[1])
        if masks is None:
            copies.append(pltpu.make_async_copy(ref, weight.at[half, :, cols], sem.at[len(copies)]))
            continue
        for block, mask in enumerate(masks):
            start = pl.multiple_of((place ^ mask) * rows, 16)
            copies.append(
                pltpu.make_async_copy(
                    ref.at[pl.ds(block * rows, rows)],
                    weight.at[half, pl.ds(start, rows), cols],
                    sem.at[len(copies)],
                )
            )
    return copies


def copy_count(plan):
    return sum(1 if masks is None else len(masks) for masks, _, _ in plan)


def bias_of(column, row, run, last, length):
    key = lax.broadcasted_iota(jnp.int32, (2 * length, length), 0) - length
    query = lax.broadcasted_iota(jnp.int32, (2 * length, length), 1)
    ok = (column == row) & (key <= query) & ((key >= 0) | ((run > 0) & (run <= last)))
    return jnp.where(ok, 0.0, NEGATIVE)


def softmax_of(scores, bias):
    scores = scores * SCALE + bias
    exponent = jnp.exp(scores - jnp.max(scores, axis=0, keepdims=True))
    return exponent * (1.0 / jnp.sum(exponent, axis=0, keepdims=True))


def normalized(x, gain):
    wide = x.astype(jnp.float32)
    inverse = lax.rsqrt(jnp.mean(wide * wide, axis=-1, keepdims=True) + 1e-05)
    return wide, inverse, (wide * inverse * gain).astype(jnp.bfloat16)


def projected(normed, weight, proj, step, copies, plan, phase):
    half = weight.shape[2]
    at = 0
    for mine in (True, False):
        h = phase if mine else 1 - phase
        for masks, _, own in plan:
            if own == mine:
                for _ in range(1 if masks is None else len(masks)):
                    copies[at].wait()
                    at += 1

        def tile(n, _, h=h):
            column = pl.multiple_of(n * step, LANES)
            product = jnp.dot(normed[...], weight[h, :, pl.ds(column, step)], preferred_element_type=jnp.float32)
            proj[:, pl.ds(pl.multiple_of(h * half + column, LANES), step)] = product.astype(jnp.bfloat16)
            return 0

        lax.fori_loop(0, half // step, tile, 0)


def grouped(count=8):
    return [range(h, min(h + count, HEADS)) for h in range(0, HEADS, count)]


def forward_kernel(plan, shard_rows, runs, first_run, *refs):
    count = len(plan)
    at_ref, column_ref, row_ref, gain_ref = refs[:4]
    tokens, pieces = refs[4 : 4 + runs], refs[4 + runs : 4 + runs + count]
    refs = refs[4 + runs + count :]
    outs, kept_ref = refs[: runs - 1], refs[runs - 1]
    weight, proj_ref, normed_ref, total, sem, kept_sem = refs[runs:]
    phase, place = at_ref[0], at_ref[1]
    copies = fetch(plan, pieces, weight, sem, place, phase, shard_rows)
    for c in copies:
        c.start()
    length, width = row_ref.shape[2], weight.shape[1]
    for i in range(runs):
        normed_ref[i * length : (i + 1) * length] = normalized(tokens[i][...], gain_ref[...])[2]
    projected(normed_ref, weight, proj_ref, width // 2, copies, plan, phase)
    keep = pltpu.make_async_copy(proj_ref, kept_ref, kept_sem)
    keep.start()

    for i in range(1, runs):
        queries, keys = slice(i * length, (i + 1) * length), slice((i - 1) * length, (i + 1) * length)
        here = first_run + 2 + i
        label = slice((here - 1) * length, (here + 1) * length)
        bias = bias_of(column_ref[label], row_ref[here], place + i + first_run, at_ref[2], length)
        total[...] = tokens[i][...].astype(jnp.float32)
        for heads in grouped():
            wins = [window(head, width) for head in heads]
            scores = []
            for cols, own in wins:
                q = only(own, proj_ref[queries, cols])
                scores.append(dot(proj_ref[keys, width + cols.start : width + cols.stop], q, (1, 1)))
            soft = [softmax_of(x, bias).astype(jnp.bfloat16) for x in scores]
            for (cols, own), p in zip(wins, soft):
                v = proj_ref[keys, 2 * width + cols.start : 2 * width + cols.stop]
                total[:, cols] += dot(p, only(own, v), (0, 0))
        outs[i - 1][...] = total[...].astype(jnp.bfloat16)
    keep.wait()


def backward_kernel(plan, shard_rows, runs, first_run, fresh, *refs):
    count, given = len(plan), 2 * runs - 1
    at_ref, column_ref, row_ref, gain_ref = refs[:4]
    arrays, pieces = refs[4 : 4 + given], refs[4 + given : 4 + given + count]
    refs = refs[4 + given + count :]
    length = row_ref.shape[2]

    def part(at, cols=slice(None)):
        return arrays[at][:, cols]

    if fresh:
        grad_ref, term_ref, out_ref, weight, proj_ref, normed_ref, dq, dk, dv, total, sem = refs
    else:
        proj_ref, grad_ref, term_ref, weight, dq, dk, dv, total, sem = refs
    phase, place = at_ref[0], at_ref[1]
    copies = fetch(plan, pieces, weight, sem, place, phase, shard_rows)
    for c in copies:
        c.start()
    width = weight.shape[1]
    dq[...] = jnp.zeros_like(dq)
    dk[...] = jnp.zeros_like(dk)
    dv[...] = jnp.zeros_like(dv)
    if fresh:
        for i in range(runs):
            normed_ref[i * length : (i + 1) * length] = normalized(part(i), gain_ref[...])[2]
        projected(normed_ref, weight, proj_ref, width // 2, copies, plan, phase)

    for i in range(1, runs):
        inner, last, attend = i > 1, i == runs - 1, fresh and i == 1
        queries, keys = slice(i * length, (i + 1) * length), slice((i - 1) * length, (i + 1) * length)
        upstream = slice((i - 1) * length, i * length)
        lo, hi = (0 if inner else length), (length if last else 2 * length)
        into = slice((i - 2) * length + lo, (i - 2) * length + hi)
        label = slice((first_run + 2 + i - 1) * length, (first_run + 2 + i + 1) * length)
        bias = bias_of(column_ref[label], row_ref[first_run + 2 + i], place + i + first_run, at_ref[2], length)
        if attend:
            total[0:length] = part(i).astype(jnp.float32)
        for heads in grouped():
            wins = [window(head, width) for head in heads]
            staged = []
            for cols, own in wins:
                q = only(own, proj_ref[queries, cols])
                g = only(own, part(runs + i - 1, cols))
                k = proj_ref[keys, width + cols.start : width + cols.stop]
                v = proj_ref[keys, 2 * width + cols.start : 2 * width + cols.stop]
                staged.append((q, g, dot(k, q, (1, 1)), dot(v, g, (1, 1))))
            graded = []
            for q, g, scores, grad_soft in staged:
                soft = softmax_of(scores, bias)
                weighed = soft * grad_soft
                grads = (weighed - soft * jnp.sum(weighed, axis=0, keepdims=True)) * SCALE
                graded.append((q, g, soft.astype(jnp.bfloat16), grads.astype(jnp.bfloat16)))
            for (cols, own), (q, g, soft, grads) in zip(wins, graded):
                dv[into, cols] += dot(soft[lo:hi], g, (1, 0))
                dk[into, cols] += dot(grads[lo:hi], q, (1, 0))
                if not last:
                    k = proj_ref[keys, width + cols.start : width + cols.stop]
                    dq[upstream, cols] += dot(grads, only(own, k), (0, 0))
                if attend:
                    v = proj_ref[keys, 2 * width + cols.start : 2 * width + cols.stop]
                    total[0:length, cols] += dot(soft, only(own, v), (0, 0))
        if attend:
            out_ref[...] = total[0:length].astype(jnp.bfloat16)

    if not fresh:
        for c in copies:
            c.wait()
    half = weight.shape[2]
    step = width // 2
    for tile in range(3 * width // step):
        source, column = divmod(tile * step, width)
        grads = (dq, dk, dv)[source][:, column : column + step].astype(jnp.bfloat16)
        start = tile * step % half
        product = dot(grads, weight[tile * step // half, :, start : start + step], (1, 1))
        if tile == 0:
            total[...] = product
        else:
            total[...] += product
    for i in range(1, runs - 1):
        rows = slice((i - 1) * length, i * length)
        wide, inverse, _ = normalized(part(i), gain_ref[...])
        grad_normed = total[rows]
        if i == 1:
            term_ref[...] = jnp.sum(grad_normed * wide * inverse, axis=0, keepdims=True)
        scaled = grad_normed * gain_ref[...]
        inner = jnp.mean(scaled * wide, axis=-1, keepdims=True)
        grads = inverse * (scaled - wide * inverse * inverse * inner)
        grad_ref[rows] = (part(runs + i - 1).astype(jnp.float32) + grads).astype(jnp.bfloat16)


def specs(*kinds):
    spaces = {"s": pltpu.SMEM, "v": pltpu.VMEM, "a": pl.ANY}
    return [pl.BlockSpec(memory_space=spaces[k]) for k in kinds]


def flattened(found):
    arrays, plan = [], []
    for array, masks, column in found:
        arrays.append(array)
        plan.append((masks, column, True))
    for array, masks, column in found:
        arrays.append(traded(array, "phase", 1))
        plan.append((masks, column, False))
    return arrays, plan


def shards(tokens, segment_ids, loss_mask, qkv_weight, gains, cotangent):
    length, width = tokens.shape[1:]
    phase = lax.axis_index("phase")
    place = lax.axis_index("dp")
    shard_rows, columns = qkv_weight.shape[1:]
    half = columns // 2
    first = phase == 0
    lo, hi = qkv_weight[0, :, :half], qkv_weight[0, :, half:]
    swapped = traded(jnp.where(first, hi, lo), "phase", 1)
    cut = half * 2 // 5 // LANES * LANES
    w0, plan0 = flattened(gathered(jnp.where(first, lo, swapped), "dp", half, False))
    w1, plan1 = flattened(gathered(jnp.where(first, swapped, hi), "dp", cut, True))

    mine = lambda a: jnp.where(first, a[0], a[1])
    x = mine(tokens)
    g2 = jnp.where(mine(loss_mask)[:, None] == 1, mine(cotangent), jnp.zeros((), jnp.bfloat16))
    right, left = passed_along(x, "dp", -1), passed_along(x, "dp", 1)
    upstream = (g2, passed_along(g2, "dp", -1))
    runs = 5
    labels = lax.dynamic_slice_in_dim(jnp.pad(mine(segment_ids), 2 * length), place * length, runs * length)
    column = labels[:, None]
    row = labels.reshape(runs, 1, length)
    other = traded(gains, "phase", 1)
    gain0, gain1 = jnp.where(first, gains, other), jnp.where(first, other, gains)
    at = jnp.stack([phase, place, jnp.int32(lax.axis_size("dp") - 1)]).astype(jnp.int32)
    limit = pltpu.CompilerParams(vmem_limit_bytes=32 * 1024 * 1024)
    bf16, f32 = jnp.bfloat16, jnp.float32
    weight_scratch = pltpu.VMEM((2, width, half), bf16)
    matmul = 2 * width * columns

    labelled = (column, row)
    estimate = pl.CostEstimate(
        flops=2 * matmul * runs * length, bytes_accessed=2 * width * columns, transcendentals=0
    )
    near = (left, x, right)
    rows = len(near) * length
    h1, h1_next, proj0 = pl.pallas_call(
        functools.partial(forward_kernel, plan0, shard_rows, len(near), -1),
        out_shape=(
            jax.ShapeDtypeStruct((length, width), bf16),
            jax.ShapeDtypeStruct((length, width), bf16),
            jax.ShapeDtypeStruct((rows, columns), bf16),
        ),
        in_specs=specs(*"svvv", *("v" * len(near)), *("a" * len(w0))),
        out_specs=tuple(specs(*"vva")),
        scratch_shapes=[
            weight_scratch,
            pltpu.VMEM((rows, columns), bf16),
            pltpu.VMEM((rows, width), bf16),
            pltpu.VMEM((length, width), f32),
            pltpu.SemaphoreType.DMA((copy_count(plan0),)),
            pltpu.SemaphoreType.DMA,
        ],
        compiler_params=limit,
        cost_estimate=estimate,
        name="forward0",
    )(at, *labelled, gain0, *near, *w0)
    around = (passed_along(h1, "dp", 1), h1, h1_next)

    def backward(arrays, gain, weights, plan, proj):
        fresh = proj is None
        runs = (len(arrays) + 1) // 2
        outs = (runs - 2) * length
        shapes = [jax.ShapeDtypeStruct((outs, width), bf16), jax.ShapeDtypeStruct((1, width), f32)]
        scratch = [weight_scratch]
        if fresh:
            shapes.append(jax.ShapeDtypeStruct((length, width), bf16))
            scratch += [pltpu.VMEM((runs * length, columns), bf16), pltpu.VMEM((runs * length, width), bf16)]
        scratch += [pltpu.VMEM((outs, width), f32)] * 4
        scratch.append(pltpu.SemaphoreType.DMA((copy_count(plan),)))
        kinds = "svvv" + "v" * len(arrays) + "a" * len(weights) + ("" if fresh else "v")
        return pl.pallas_call(
            functools.partial(backward_kernel, plan, shard_rows, runs, -1, fresh),
            out_shape=tuple(shapes),
            in_specs=specs(*kinds),
            out_specs=tuple(specs(*("v" * len(shapes)))),
            scratch_shapes=scratch,
            compiler_params=limit,
            cost_estimate=estimate,
            name="backward1" if fresh else "backward0",
        )(at, *labelled, gain, *arrays, *weights, *(() if fresh else (proj,)))

    g1, term1, out = backward((*around, *upstream), gain1, w1, plan1, None)
    g1_next = passed_along(g1, "dp", -1)
    g0, term0 = backward((*near, g1, g1_next), gain0, w0, plan0, proj0)
    received = traded(jnp.where(first, out, g0), "phase", 1)
    boundary = jnp.where(first, jnp.stack([g0, received]), jnp.stack([received, out]))[None]
    terms = jnp.where(first, term0, term1) + traded(jnp.where(first, term1, term0), "phase", 1)
    size = lax.axis_size("dp")
    if size & (size - 1):
        return boundary, lax.psum_scatter(terms, "dp", scatter_dimension=1, tiled=True)
    terms = terms.reshape(size, width // size)
    bit = size // 2
    while bit:
        if bit == 1:
            terms, boundary = lax.optimization_barrier((terms, boundary))
        upper = (place & bit) != 0
        low, high = terms[:bit], terms[bit:]
        terms = jnp.where(upper, high, low) + traded(jnp.where(upper, low, high), "dp", bit)
        bit //= 2
    return boundary, terms


def solution(mesh):
    in_specs = (
        P(None, "dp", None),
        P(),
        P(None, "dp"),
        P("phase", "dp", None),
        P("phase", None),
        P(None, "dp", None),
    )
    out_specs = (P("phase", None, "dp", None), P("phase", "dp"))
    return jax.shard_map(shards, mesh=mesh, in_specs=in_specs, out_specs=out_specs, check_vma=False)
```
